32 devices in a mesh: occi: 4 (over y, x), occj: 8 (over z, core).
Axes of the slice: x: 2, y: 2, z: 4, core: 2. Of those that a mesh axis runs over, the one named last changes fastest.
Arguments:
- amplitudes: bfloat16 [8, 8, 512, 512], P('occi', 'occj'), may hold values from -6 to 6
- exch_int: bfloat16 [8, 8, 512, 512], P('occi', 'occj'), may hold values from -6 to 6
- thc_factor: bfloat16 [512, 2048], replicated, may hold values from -0.25 to 0.25
- thc_core: bfloat16 [2048, 2048], replicated, may hold values from -1.5 to 1.5
- fock_vir: bfloat16 [512, 512], replicated, may hold values from -0.25 to 0.25
- eps_vir: float32 [512], replicated, may hold values from 0.5 to 3
- eps_occ: float32 [8], replicated, may hold values from -1.5 to -0.2
- fock_occ: float32 [8, 8], replicated, may hold values from -1.8 to 1.8
- couple_list: int32 [8, 6], replicated, may hold values from 0 to 7, as said below
- couple_count: int32 [8], replicated, may hold values from 1 to 6, as said below
Outputs:
- residual: float32 [8, 8, 512, 512], P('occi', 'occj')
- amplitudes_new: bfloat16 [8, 8, 512, 512], P('occi', 'occj')
The draws below stay inside these ranges and needn't reach their ends.
Inputs may be any that keep to these rules, and one draw needn't show every extreme that they name: `couple_list`: row j holds 6 distinct orbitals, none of them j. `couple_count`: some row uses all 6 entries.
All inputs are finite; a program needn't handle non-finite values.
Results may differ from the reference program's by a relative error of at most 0.0045.
Values may be sent and summed in bfloat16 or wider, within the bound.
A program may use at most 128 MiB of HBM per device.

```python
import math
import jax
import jax.numpy as jnp
from jax import lax

V = 512
RANK = 2048
LMAX = 6
NO = 8


def draw_couple_list(key, part):
    scores = jax.random.randint(jax.random.fold_in(key, 11), (NO, NO), 0, 2 ** 20)
    ranked = scores * NO + jnp.arange(NO, dtype=jnp.int32)[None, :]
    ranked = jnp.where(jnp.eye(NO, dtype=bool), 2 ** 30, ranked)
    ordering = jnp.argsort(ranked, axis=1, stable=True)
    return ordering[:, :LMAX].astype(jnp.int32)


def draw_couple_count(key, part):
    counts = jax.random.randint(jax.random.fold_in(key, 23), (NO,), 1, LMAX + 1)
    heaviest = jax.random.randint(jax.random.fold_in(key, 29), (), 0, NO)
    return jnp.where(jnp.arange(NO) == heaviest, LMAX, counts).astype(jnp.int32)


def block_scale(key, extent, split, least, largest):
    def one(axis_at, shards_of):
        steps = jax.random.uniform(jax.random.fold_in(jax.random.fold_in(key, 6), axis_at), (shards_of,), jnp.float32, least / len(split), largest / len(split))
        return jnp.repeat(jnp.exp(steps), extent[axis_at] // shards_of).reshape((-1,) + (1,) * (len(extent) - axis_at - 1))

    factor_of = one(*split[0])
    for cut in split[1:]:
        factor_of = factor_of * one(*cut)
    return factor_of


def normal_values(rng, shape, deviation, bound, shards=(), kind=jnp.bfloat16):
    drawn = jax.random.normal(rng, shape, jnp.float32) * deviation
    if len(shards) > 0:
        drawn = block_scale(rng, shape, shards, -0.22, 0.18) * drawn
    return jnp.clip(drawn, min=-bound, max=bound).astype(kind)


def setup_inputs(seed: int = 0) -> dict:
    seeds = jax.random.split(jax.random.key(seed), 11)
    return {
        "amplitudes": normal_values(seeds[0], (NO, NO, V, V), 1.0, 6.0, ((0, 4), (1, 8))),
        "exch_int": normal_values(seeds[1], (NO, NO, V, V), 1.0, 6.0, ((0, 4), (1, 8))),
        "thc_factor": normal_values(seeds[2], (V, RANK), V ** -0.5, 0.25),
        "thc_core": normal_values(seeds[3], (RANK, RANK), 0.25, 1.5),
        "fock_vir": normal_values(seeds[4], (V, V), V ** -0.5, 0.25),
        "eps_vir": jnp.clip(jnp.exp(jax.random.uniform(seeds[5], (V,), jnp.float32, math.log(0.5), math.log(3.0))), 0.5, 3.0),
        "eps_occ": jnp.clip(jax.random.uniform(seeds[6], (NO,), jnp.float32, -1.5, -0.2), -1.5, -0.2),
        "fock_occ": normal_values(seeds[7], (NO, NO), 0.3, 1.8, (), jnp.float32),
        "couple_list": draw_couple_list(jax.random.fold_in(seeds[10], 71), 0),
        "couple_count": draw_couple_count(jax.random.fold_in(seeds[10], 71), 0),
    }


def coupling(fock_occ, couple_list, couple_count):
    n_occ = fock_occ.shape[0]
    slots = jnp.arange(couple_list.shape[1], dtype=jnp.int32)
    active = slots[None, :] < couple_count[:, None]
    target = jnp.arange(n_occ, dtype=jnp.int32)
    hits = (couple_list[:, :, None] == target[None, None, :]) & active[:, :, None]
    return fock_occ * jnp.sum(hits.astype(fock_occ.dtype), axis=1)


def pair_terms(amp_pair, integral, thc_factor, thc_core, fock_vir):
    first = jnp.dot(amp_pair, thc_factor, preferred_element_type=jnp.float32).astype(jnp.bfloat16)
    middle = lax.dot_general(thc_factor, first, (((0,), (0,)), ((), ())), preferred_element_type=jnp.float32)
    scaled = (thc_core.astype(jnp.float32) * middle).astype(jnp.bfloat16)
    second = jnp.dot(thc_factor, scaled, preferred_element_type=jnp.float32).astype(jnp.bfloat16)
    ladder = lax.dot_general(second, thc_factor, (((1,), (1,)), ((), ())), preferred_element_type=jnp.float32)
    virtual = jnp.dot(fock_vir, amp_pair, preferred_element_type=jnp.float32)
    return integral.astype(jnp.float32) + ladder + virtual


def reference(amplitudes, exch_int, thc_factor, thc_core, fock_vir, eps_vir, eps_occ, fock_occ, couple_list, couple_count):
    n_occ = amplitudes.shape[0]
    virt = amplitudes.shape[2]
    weights = coupling(fock_occ, couple_list, couple_count)
    flat_amps = amplitudes.reshape(n_occ * n_occ, virt, virt)
    flat_ints = exch_int.reshape(n_occ * n_occ, virt, virt)
    local_terms = lax.map(lambda pair_in: pair_terms(pair_in[0], pair_in[1], thc_factor, thc_core, fock_vir), (flat_amps, flat_ints))
    local_terms = local_terms.reshape(n_occ, n_occ, virt, virt)

    def occupied_row(row_amps):
        return -jnp.einsum('jk,kab->jab', weights, row_amps.astype(jnp.float32), precision=lax.Precision.HIGHEST)

    occupied = lax.map(occupied_row, amplitudes)
    half = local_terms + occupied
    residual = half + jnp.transpose(half, (1, 0, 3, 2))
    denominator = eps_vir[None, None, :, None] + eps_vir[None, None, None, :] - eps_occ[:, None, None, None] - eps_occ[None, :, None, None]
    updated = (amplitudes.astype(jnp.float32) - residual / denominator).astype(jnp.bfloat16)
    return residual, updated
```

```python
import jax
import jax.numpy as jnp
from jax import lax
from jax.sharding import PartitionSpec as P


def coupling(fock_occ, couple_list, couple_count):
    n_occ = fock_occ.shape[0]
    slots = jnp.arange(couple_list.shape[1], dtype=jnp.int32)
    active = slots[None, :] < couple_count[:, None]
    target = jnp.arange(n_occ, dtype=jnp.int32)
    hits = (couple_list[:, :, None] == target[None, None, :]) & active[:, :, None]
    return fock_occ * jnp.sum(hits.astype(fock_occ.dtype), axis=1)


def pair_terms(amp_pair, integral, thc_factor, thc_core, fock_vir):
    first = jnp.dot(amp_pair, thc_factor, preferred_element_type=jnp.float32).astype(jnp.bfloat16)
    middle = lax.dot_general(
        thc_factor, first, (((0,), (0,)), ((), ())), preferred_element_type=jnp.float32
    )
    scaled = (thc_core * middle).astype(jnp.bfloat16)
    second = jnp.dot(thc_factor, scaled, preferred_element_type=jnp.float32).astype(jnp.bfloat16)
    ladder = lax.dot_general(
        second, thc_factor, (((1,), (1,)), ((), ())), preferred_element_type=jnp.float32
    )
    virtual = jnp.dot(fock_vir, amp_pair, preferred_element_type=jnp.float32)
    return integral.astype(jnp.float32) + ladder + virtual


def shards(
    amplitudes,
    exch_int,
    thc_factor,
    thc_core,
    fock_vir,
    eps_vir,
    eps_occ,
    fock_occ,
    couple_list,
    couple_count,
):
    rows_i = amplitudes.shape[0]
    virt = amplitudes.shape[2]
    n_first = lax.axis_size("occi")
    n_second = lax.axis_size("occj")
    first_index = lax.axis_index("occi")
    second_index = lax.axis_index("occj")
    weights = coupling(fock_occ, couple_list, couple_count)
    pairs_here = amplitudes.reshape(rows_i, virt, virt)
    integrals = exch_int.reshape(rows_i, virt, virt)
    row_weights = lax.dynamic_slice_in_dim(weights, second_index, 1, 0)[0]
    gathered = lax.all_gather(amplitudes, "occj", axis=1, tiled=True)
    ladders = [
        pair_terms(pairs_here[s], integrals[s], thc_factor, thc_core, fock_vir)
        for s in range(rows_i)
    ]
    half = jnp.stack(ladders)
    for k in range(n_second):
        half = half - row_weights[k] * gathered[:, k].astype(jnp.float32)
    turned = half.astype(jnp.bfloat16).transpose(0, 2, 1)
    mirrored = jnp.zeros_like(turned)
    for t in range(rows_i):
        hops = []
        for a in range(n_first):
            for j in range(n_second):
                s = (j + t) % rows_i
                hops.append((a * n_second + j, (j // rows_i) * n_second + a * rows_i + s))
        sent = lax.dynamic_index_in_dim(turned, (second_index + t) % rows_i, 0, keepdims=False)
        got = lax.ppermute(sent, ("occi", "occj"), hops)
        mirrored = lax.dynamic_update_index_in_dim(
            mirrored, got, (second_index + rows_i - t) % rows_i, 0
        )
    residual = half + mirrored.astype(jnp.float32)
    occ_rows = lax.dynamic_slice_in_dim(eps_occ, first_index * rows_i, rows_i, 0)
    occ_column = lax.dynamic_slice_in_dim(eps_occ, second_index, 1, 0)
    denominator = (
        eps_vir[None, :, None] + eps_vir[None, None, :] - occ_rows[:, None, None] - occ_column[0]
    )
    updated = (pairs_here.astype(jnp.float32) - residual / denominator).astype(jnp.bfloat16)
    return (residual.reshape(rows_i, 1, virt, virt), updated.reshape(rows_i, 1, virt, virt))


def solution(mesh):
    placed = (P("occi", "occj", None, None),) * 2 + (P(),) * 8
    return jax.shard_map(
        shards,
        mesh=mesh,
        in_specs=placed,
        out_specs=(P("occi", "occj", None, None), P("occi", "occj", None, None)),
        check_vma=False,
    )
```

```python
import functools

import jax
import jax.numpy as jnp
from jax import lax
from jax.experimental import pallas as pl
from jax.experimental.pallas import tpu as pltpu
from jax.sharding import PartitionSpec as P

MESH = pl.DeviceIdType.MESH
F32 = jnp.float32
BF16 = jnp.bfloat16


def coupling(fock_occ, couple_list, couple_count):
    n_occ = fock_occ.shape[0]
    slots = jnp.arange(couple_list.shape[1], dtype=jnp.int32)
    active = slots[None, :] < couple_count[:, None]
    target = jnp.arange(n_occ, dtype=jnp.int32)
    hits = (couple_list[:, :, None] == target[None, None, :]) & active[:, :, None]
    return fock_occ * jnp.sum(hits.astype(fock_occ.dtype), axis=1)


def tile_of(extent):
    return 512 if extent % 512 == 0 else extent


def kernel(
    n_first,
    n_second,
    amp_hbm,
    int_hbm,
    x_hbm,
    core_hbm,
    fock_hbm,
    weight_ref,
    occ_ref,
    row_ref,
    column_ref,
    residual_ref,
    updated_ref,
    pool,
    integral,
    x,
    xt,
    core,
    fock,
    first,
    scaled,
    half,
    part_out,
    part_in,
    turned,
    mirror,
    local_sem,
    gsend_sem,
    grecv_sem,
    relay_sem,
    psend_sem,
    precv_sem,
    msend_sem,
    mrecv_sem,
):
    rows, virt = half.shape[0], half.shape[1]
    rank = x.shape[1]
    near = n_second // 2
    tile = tile_of(rank)
    tiles = rank // tile
    chunk = 128
    a = lax.axis_index("occi")
    j = lax.axis_index("occj")
    mine = lax.rem(j, near)
    base = j - mine
    across = lax.rem(j + near, n_second)
    i_half = a // (n_first // 2)
    diagonal = i_half == j // near
    partner = mine + 1 - 2 * lax.rem(mine, 2)
    slot = lax.rem(j, rows)

    def signal(first_coord, second_coord):
        pl.semaphore_signal(
            pltpu.get_barrier_semaphore(),
            inc=1,
            device_id=(first_coord, second_coord),
            device_id_type=MESH,
        )

    for d in range(1, near):
        signal(a, base + lax.rem(mine + d, near))
    signal(a, across)
    for s in range(rows):
        pair_i = a * rows + s

        @pl.when(diagonal)
        def _():
            signal(across // rows, pair_i)

        @pl.when(jnp.logical_not(diagonal))
        def _():
            signal(j // rows, lax.rem(pair_i + near, n_second))

        @pl.when(pair_i != j)
        def _():
            signal(j // rows, pair_i)

    loads = [
        pltpu.make_async_copy(x_hbm, x, local_sem.at[0]),
        pltpu.make_async_copy(fock_hbm, fock, local_sem.at[1]),
        pltpu.make_async_copy(int_hbm, integral, local_sem.at[2]),
        pltpu.make_async_copy(core_hbm, core, local_sem.at[3]),
    ]
    own_loads = [
        pltpu.make_async_copy(amp_hbm.at[s], pool.at[s, mine], local_sem.at[4 + s])
        for s in range(rows)
    ]
    for load in own_loads + loads:
        load.start()
    self_pair = a == j // rows
    greeted = near + 2 * rows

    @pl.when(self_pair)
    def _():
        pl.semaphore_wait(pltpu.get_barrier_semaphore(), greeted - 1)

    @pl.when(jnp.logical_not(self_pair))
    def _():
        pl.semaphore_wait(pltpu.get_barrier_semaphore(), greeted)

    def gather_copy(s, d):
        peer = lax.rem(mine + d, near)
        return pltpu.make_async_remote_copy(
            src_ref=amp_hbm.at[s],
            dst_ref=pool.at[s, mine],
            send_sem=gsend_sem.at[s, d],
            recv_sem=grecv_sem.at[s, mine],
            device_id=(a, base + peer),
            device_id_type=MESH,
        )

    def partner_copy(s):
        return pltpu.make_async_remote_copy(
            src_ref=amp_hbm.at[s],
            dst_ref=pool.at[s, mine],
            send_sem=gsend_sem.at[s, 0],
            recv_sem=grecv_sem.at[s, mine],
            device_id=(a, base + partner),
            device_id_type=MESH,
        )

    def arrived(s, origin):
        pltpu.make_async_remote_copy(
            src_ref=amp_hbm.at[s],
            dst_ref=pool.at[s, origin],
            send_sem=gsend_sem.at[s, 0],
            recv_sem=grecv_sem.at[s, origin],
            device_id=(a, base + partner),
            device_id_type=MESH,
        ).wait_recv()

    def relay_copy(s, d):
        origin = lax.rem(mine + d, near)
        return pltpu.make_async_remote_copy(
            src_ref=pool.at[s, origin],
            dst_ref=pool.at[s, origin],
            send_sem=relay_sem.at[s, d],
            recv_sem=grecv_sem.at[s, origin],
            device_id=(a, base + partner),
            device_id_type=MESH,
        )

    far = range(2, near, 2)
    for s in range(rows):
        for d in far:
            gather_copy(s, d).start()
        partner_copy(s).start()

    loads[0].wait()
    for r in range(0, rank, tile):
        xt[pl.ds(r, tile), :] = x[:, pl.ds(r, tile)].T
    for load in own_loads + loads[1:3]:
        load.wait()
    for s in range(rows):
        half[s] = integral[s].astype(F32) + jnp.dot(
            fock[...], pool[s, mine], preferred_element_type=F32
        )
    loads[3].wait()

    def relay(s):
        for d in far:
            arrived(s, lax.rem(mine + d, near))
            relay_copy(s, d).start()

    def part_copy(s, to_mirror):
        if to_mirror:
            where, there = (across // rows, a * rows + s), lax.rem(across, rows)
        else:
            where, there = (a, across), s
        return pltpu.make_async_remote_copy(
            src_ref=part_out.at[s],
            dst_ref=part_in.at[there],
            send_sem=psend_sem.at[s],
            recv_sem=precv_sem.at[there],
            device_id=where,
            device_id_type=MESH,
        )

    def partial_sums(s):
        arrived(s, base * 0 + partner)
        for d in far:
            arrived(s, lax.rem(partner + near + d, near))

        @pl.loop(0, virt // chunk)
        def _(r):
            at = pl.ds(pl.multiple_of(r * chunk, chunk), chunk)
            own = jnp.zeros((chunk, virt), F32)
            other = jnp.zeros((chunk, virt), F32)
            for k in range(near):
                block = pool[s, k, at, :].astype(F32)
                own = own + weight_ref[0, k] * block
                other = other + weight_ref[1, k] * block
            half[s, at, :] = half[s, at, :] - own

            @pl.when(diagonal)
            def _():
                part_out[s, :, at] = other.T.astype(BF16)

            @pl.when(jnp.logical_not(diagonal))
            def _():
                part_out[s, at, :] = other.astype(BF16)

        @pl.when(diagonal)
        def _():
            part_copy(s, True).start()

        @pl.when(jnp.logical_not(diagonal))
        def _():
            part_copy(s, False).start()

    def mirror_copy(s):
        return pltpu.make_async_remote_copy(
            src_ref=turned.at[s],
            dst_ref=mirror.at[slot],
            send_sem=msend_sem.at[s],
            recv_sem=mrecv_sem.at[slot],
            device_id=(j // rows, a * rows + s),
            device_id_type=MESH,
        )

    def mirror_arrival(s):
        return pltpu.make_async_remote_copy(
            src_ref=turned.at[s],
            dst_ref=mirror.at[s],
            send_sem=msend_sem.at[s],
            recv_sem=mrecv_sem.at[s],
            device_id=(j // rows, a * rows + s),
            device_id_type=MESH,
        )

    def part_arrival(s):
        return pltpu.make_async_remote_copy(
            src_ref=part_out.at[s],
            dst_ref=part_in.at[s],
            send_sem=psend_sem.at[s],
            recv_sem=precv_sem.at[s],
            device_id=(a, across),
            device_id_type=MESH,
        )

    def send_half(s):
        part_arrival(s).wait_recv()

        @pl.loop(0, virt // chunk)
        def _(r):
            at = pl.ds(pl.multiple_of(r * chunk, chunk), chunk)
            rest = half[s, at, :] - part_in[s, at, :].astype(F32)
            half[s, at, :] = rest
            turned[s, :, at] = rest.T.astype(BF16)

        @pl.when(a * rows + s != j)
        def _():
            mirror_copy(s).start()

    steps = rows * tiles
    relay_at, sums_at, half_at = 1, min(3, steps - 1), min(tiles + 1, steps - 1)

    @pl.loop(0, steps)
    def _(step):
        s = lax.rem(j + step // tiles, rows)
        q = lax.rem(step, tiles)
        at_q = pl.ds(pl.multiple_of(q * tile, tile), tile)

        @pl.when(step == relay_at)
        def _():
            relay(0)

        @pl.when(step == relay_at + 1)
        def _():
            for s in range(1, rows):
                relay(s)

        @pl.when(step == sums_at)
        def _():
            @pl.loop(0, rows)
            def _(t):
                partial_sums(lax.rem(j + t, rows))

        @pl.when(jnp.logical_and(step == half_at, jnp.logical_not(diagonal)))
        def _():
            send_half(slot)

        first[...] = jnp.dot(
            pool[s, mine], x[:, at_q], preferred_element_type=F32
        ).astype(BF16)

        @pl.loop(0, tiles)
        def _(p):
            at_p = pl.ds(pl.multiple_of(p * tile, tile), tile)
            middle = jnp.dot(xt[at_p, :], first[...], preferred_element_type=F32)
            scaled[at_p, :] = (core[at_p, at_q].astype(F32) * middle).astype(BF16)

        second = jnp.dot(x[...], scaled[...], preferred_element_type=F32).astype(BF16)
        half[s] += lax.dot_general(
            second, x[:, at_q], (((1,), (1,)), ((), ())), preferred_element_type=F32
        )

    @pl.when(diagonal)
    def _():
        send_half(slot)

    @pl.loop(1, rows)
    def _(t):
        send_half(lax.rem(j + t, rows))

    @pl.loop(0, rows)
    def _(t):
        s = lax.rem(j + t, rows)
        local = a * rows + s == j

        def finish(source):
            @pl.loop(0, virt // chunk)
            def _(r):
                at = pl.ds(pl.multiple_of(r * chunk, chunk), chunk)
                total = half[s, at, :] + source[s, at, :].astype(F32)
                residual_ref[s, at, :] = total
                denominator = column_ref[at, :] + row_ref[...] - occ_ref[0, s] - occ_ref[1, s]
                updated_ref[s, at, :] = (
                    pool[s, mine, at, :].astype(F32) - total / denominator
                ).astype(BF16)

        @pl.when(local)
        def _():
            finish(turned)

        @pl.when(jnp.logical_not(local))
        def _():
            mirror_arrival(s).wait_recv()
            finish(mirror)
            mirror_copy(s).wait_send()

    for s in range(rows):
        for d in far:
            gather_copy(s, d).wait_send()
            relay_copy(s, d).wait_send()
        partner_copy(s).wait_send()
        part_arrival(s).wait_send()


def shards(
    amplitudes,
    exch_int,
    thc_factor,
    thc_core,
    fock_vir,
    eps_vir,
    eps_occ,
    fock_occ,
    couple_list,
    couple_count,
):
    rows = amplitudes.shape[0]
    virt = amplitudes.shape[2]
    rank = thc_factor.shape[1]
    n_first = lax.axis_size("occi")
    n_second = lax.axis_size("occj")
    near = n_second // 2
    a = lax.axis_index("occi")
    j = lax.axis_index("occj")
    weights = coupling(fock_occ, couple_list, couple_count)
    start = (j // near) * near
    own = lax.dynamic_slice(weights, (j, start), (1, near))
    other = lax.dynamic_slice(weights, ((j + near) % n_second, start), (1, near))
    weight = jnp.concatenate([own, other])
    occ = jnp.stack(
        [
            lax.dynamic_slice_in_dim(eps_occ, a * rows, rows, 0),
            jnp.broadcast_to(lax.dynamic_slice_in_dim(eps_occ, j, 1, 0), (rows,)),
        ]
    )
    anywhere = pl.BlockSpec(memory_space=pl.ANY)
    vmem = pl.BlockSpec(memory_space=pltpu.VMEM)
    smem = pl.BlockSpec(memory_space=pltpu.SMEM)
    tile = tile_of(rank)
    pair = (rows, virt, virt)
    dma = pltpu.SemaphoreType.DMA
    residual, updated = pl.pallas_call(
        functools.partial(kernel, n_first, n_second),
        out_shape=(jax.ShapeDtypeStruct(pair, F32), jax.ShapeDtypeStruct(pair, BF16)),
        in_specs=[anywhere] * 5 + [smem, smem, vmem, vmem],
        out_specs=(vmem, vmem),
        scratch_shapes=[
            pltpu.VMEM((rows, near, virt, virt), BF16),
            pltpu.VMEM(pair, BF16),
            pltpu.VMEM((virt, rank), BF16),
            pltpu.VMEM((rank, virt), BF16),
            pltpu.VMEM((rank, rank), BF16),
            pltpu.VMEM((virt, virt), BF16),
            pltpu.VMEM((virt, tile), BF16),
            pltpu.VMEM((rank, tile), BF16),
            pltpu.VMEM(pair, F32),
            pltpu.VMEM(pair, BF16),
            pltpu.VMEM(pair, BF16),
            pltpu.VMEM(pair, BF16),
            pltpu.VMEM(pair, BF16),
            dma((4 + rows,)),
            dma((rows, near)),
            dma((rows, near)),
            dma((rows, near)),
            dma((rows,)),
            dma((rows,)),
            dma((rows,)),
            dma((rows,)),
        ],
        compiler_params=pltpu.CompilerParams(
            collective_id=0, has_side_effects=True, vmem_limit_bytes=60 * 1024 * 1024
        ),
    )(
        amplitudes.reshape(pair),
        exch_int.reshape(pair),
        thc_factor,
        thc_core,
        fock_vir,
        weight,
        occ,
        eps_vir.reshape(1, virt),
        eps_vir.reshape(virt, 1),
    )
    return (residual.reshape(rows, 1, virt, virt), updated.reshape(rows, 1, virt, virt))


def solution(mesh):
    placed = (P("occi", "occj", None, None),) * 2 + (P(),) * 8
    return jax.shard_map(
        shards,
        mesh=mesh,
        in_specs=placed,
        out_specs=(P("occi", "occj", None, None), P("occi", "occj", None, None)),
        check_vma=False,
    )
```

```python
import functools

import jax
import jax.numpy as jnp
from jax import lax
from jax.experimental import pallas as pl
from jax.experimental.pallas import tpu as pltpu
from jax.sharding import PartitionSpec as P

MESH = pl.DeviceIdType.MESH
F32 = jnp.float32
BF16 = jnp.bfloat16


def tile_of(extent):
    return 512 if extent % 512 == 0 else extent


def kernel(
    n_first,
    n_second,
    amp_hbm,
    int_hbm,
    x_hbm,
    core_hbm,
    fock_hbm,
    row_ref,
    eps_ref,
    fock_occ_ref,
    list_ref,
    count_ref,
    residual_ref,
    updated_ref,
    pool,
    integral,
    x,
    xt,
    core,
    fock,
    first,
    scaled,
    half,
    part_out,
    part_in,
    turned,
    mirror,
    passing,
    part_pass,
    local_sem,
    gsend_sem,
    grecv_sem,
    relay_sem,
    psend_sem,
    precv_sem,
    msend_sem,
    mrecv_sem,
    pass_sem,
    low_send_sem,
    low_recv_sem,
    low_pass_sem,
    low_done_sem,
):
    rows, virt = half.shape[0], half.shape[1]
    rank = x.shape[1]
    near = n_second // 2
    upper = pl.ds(0, virt // 2)
    lower = pl.ds(virt // 2, virt // 2)
    tile = tile_of(rank)
    tiles = rank // tile
    chunk = 128
    a = lax.axis_index("occi")
    j = lax.axis_index("occj")
    mine = lax.rem(j, near)
    base = j - mine
    across = lax.rem(j + near, n_second)
    i_half = a // (n_first // 2)
    diagonal = i_half == j // near
    partner = mine + 1 - 2 * lax.rem(mine, 2)
    slot = lax.rem(j, rows)
    flipped = lax.rem(a + n_first // 2, n_first)

    def weight(orbital, k):
        hits = jnp.float32(0.0)
        for entry in range(list_ref.shape[1]):
            active = jnp.logical_and(
                list_ref[orbital, entry] == k, entry < count_ref[orbital]
            )
            hits = hits + jnp.where(active, jnp.float32(1.0), jnp.float32(0.0))
        return hits * fock_occ_ref[orbital, k]

    def signal(first_coord, second_coord):
        pl.semaphore_signal(
            pltpu.get_barrier_semaphore(),
            inc=1,
            device_id=(first_coord, second_coord),
            device_id_type=MESH,
        )

    for d in range(1, near):
        signal(a, base + lax.rem(mine + d, near))
    signal(a, across)
    signal(flipped, j)
    signal(flipped, across)
    for s in range(rows):
        pair_i = a * rows + s

        @pl.when(diagonal)
        def _():
            signal(across // rows, pair_i)

        @pl.when(jnp.logical_not(diagonal))
        def _():
            signal(j // rows, lax.rem(pair_i + near, n_second))

        @pl.when(pair_i != j)
        def _():
            signal(j // rows, pair_i)

    @pl.when(diagonal)
    def _():
        signal(j // rows, flipped * rows + slot)

    @pl.when(jnp.logical_not(diagonal))
    def _():
        signal(lax.rem(j // rows + n_first // 2, n_first), a * rows + slot)

    loads = [
        pltpu.make_async_copy(x_hbm, x, local_sem.at[0]),
        pltpu.make_async_copy(fock_hbm, fock, local_sem.at[1]),
        pltpu.make_async_copy(int_hbm, integral, local_sem.at[2]),
        pltpu.make_async_copy(core_hbm, core, local_sem.at[3]),
    ]
    own_loads = [
        pltpu.make_async_copy(amp_hbm.at[s], pool.at[s, mine], local_sem.at[4 + s])
        for s in range(rows)
    ]
    for load in own_loads + loads:
        load.start()
    self_pair = a == j // rows
    greeted = near + 2 * rows + 3

    @pl.when(self_pair)
    def _():
        pl.semaphore_wait(pltpu.get_barrier_semaphore(), greeted - 1)

    @pl.when(jnp.logical_not(self_pair))
    def _():
        pl.semaphore_wait(pltpu.get_barrier_semaphore(), greeted)

    def gather_copy(s, d):
        peer = lax.rem(mine + d, near)
        return pltpu.make_async_remote_copy(
            src_ref=amp_hbm.at[s],
            dst_ref=pool.at[s, mine],
            send_sem=gsend_sem.at[s, d],
            recv_sem=grecv_sem.at[s, mine],
            device_id=(a, base + peer),
            device_id_type=MESH,
        )

    def partner_copy(s):
        return pltpu.make_async_remote_copy(
            src_ref=amp_hbm.at[s],
            dst_ref=pool.at[s, mine],
            send_sem=gsend_sem.at[s, 0],
            recv_sem=grecv_sem.at[s, mine],
            device_id=(a, base + partner),
            device_id_type=MESH,
        )

    def arrived(s, origin):
        pltpu.make_async_remote_copy(
            src_ref=amp_hbm.at[s],
            dst_ref=pool.at[s, origin],
            send_sem=gsend_sem.at[s, 0],
            recv_sem=grecv_sem.at[s, origin],
            device_id=(a, base + partner),
            device_id_type=MESH,
        ).wait_recv()

    def relay_copy(s, d):
        origin = lax.rem(mine + d, near)
        return pltpu.make_async_remote_copy(
            src_ref=pool.at[s, origin],
            dst_ref=pool.at[s, origin],
            send_sem=relay_sem.at[s, d],
            recv_sem=grecv_sem.at[s, origin],
            device_id=(a, base + partner),
            device_id_type=MESH,
        )

    far = range(2, near, 2)
    for s in range(rows):
        for d in far:
            gather_copy(s, d).start()
        partner_copy(s).start()

    loads[0].wait()
    for r in range(0, rank, tile):
        xt[pl.ds(r, tile), :] = x[:, pl.ds(r, tile)].T
    for load in own_loads + loads[1:3]:
        load.wait()
    for s in range(rows):
        half[s] = integral[s].astype(F32) + jnp.dot(
            fock[...], pool[s, mine], preferred_element_type=F32
        )
    loads[3].wait()

    def relay(s):
        for d in far:
            arrived(s, lax.rem(mine + d, near))
            relay_copy(s, d).start()

    def part_across(s):
        return pltpu.make_async_remote_copy(
            src_ref=part_out.at[s, upper],
            dst_ref=part_in.at[s, upper],
            send_sem=psend_sem.at[s],
            recv_sem=precv_sem.at[s],
            device_id=(a, across),
            device_id_type=MESH,
        )

    def part_turned(s):
        there = lax.rem(across, rows)
        return pltpu.make_async_remote_copy(
            src_ref=part_out.at[s],
            dst_ref=part_in.at[there],
            send_sem=psend_sem.at[s],
            recv_sem=precv_sem.at[there],
            device_id=(across // rows, a * rows + s),
            device_id_type=MESH,
        )

    def low_to_flip(s):
        return pltpu.make_async_remote_copy(
            src_ref=part_out.at[s, lower],
            dst_ref=part_pass.at[s],
            send_sem=low_send_sem.at[s],
            recv_sem=low_recv_sem.at[s],
            device_id=(flipped, j),
            device_id_type=MESH,
        )

    def low_on(s):
        return pltpu.make_async_remote_copy(
            src_ref=part_pass.at[s],
            dst_ref=part_in.at[s, lower],
            send_sem=low_pass_sem.at[s],
            recv_sem=low_done_sem.at[s],
            device_id=(flipped, across),
            device_id_type=MESH,
        )

    def partial_sums(s):
        arrived(s, base * 0 + partner)
        for d in far:
            arrived(s, lax.rem(partner + near + d, near))

        own_weights = [weight(j, base + k) for k in range(near)]
        other_weights = [weight(across, base + k) for k in range(near)]

        @pl.loop(0, virt // chunk)
        def _(r):
            at = pl.ds(pl.multiple_of(r * chunk, chunk), chunk)
            own = jnp.zeros((chunk, virt), F32)
            other = jnp.zeros((chunk, virt), F32)
            for k in range(near):
                block = pool[s, k, at, :].astype(F32)
                own = own + own_weights[k] * block
                other = other + other_weights[k] * block
            half[s, at, :] = half[s, at, :] - own

            @pl.when(diagonal)
            def _():
                part_out[s, :, at] = other.T.astype(BF16)

            @pl.when(jnp.logical_not(diagonal))
            def _():
                part_out[s, at, :] = other.astype(BF16)

        @pl.when(diagonal)
        def _():
            part_turned(s).start()

        @pl.when(jnp.logical_not(diagonal))
        def _():
            low_to_flip(s).start()
            part_across(s).start()

    def mirror_copy(s):
        return pltpu.make_async_remote_copy(
            src_ref=turned.at[s],
            dst_ref=mirror.at[slot],
            send_sem=msend_sem.at[s],
            recv_sem=mrecv_sem.at[slot],
            device_id=(j // rows, a * rows + s),
            device_id_type=MESH,
        )

    def pass_on():
        return pltpu.make_async_remote_copy(
            src_ref=turned.at[slot],
            dst_ref=passing,
            send_sem=msend_sem.at[slot],
            recv_sem=pass_sem.at[0],
            device_id=(flipped, j),
            device_id_type=MESH,
        )

    def pass_end():
        return pltpu.make_async_remote_copy(
            src_ref=passing,
            dst_ref=mirror.at[slot],
            send_sem=pass_sem.at[1],
            recv_sem=mrecv_sem.at[slot],
            device_id=(j // rows, flipped * rows + slot),
            device_id_type=MESH,
        )

    def mirror_arrival(s):
        return pltpu.make_async_remote_copy(
            src_ref=turned.at[s],
            dst_ref=mirror.at[s],
            send_sem=msend_sem.at[s],
            recv_sem=mrecv_sem.at[s],
            device_id=(j // rows, a * rows + s),
            device_id_type=MESH,
        )

    def part_arrival(s):
        return pltpu.make_async_remote_copy(
            src_ref=part_out.at[s],
            dst_ref=part_in.at[s],
            send_sem=psend_sem.at[s],
            recv_sem=precv_sem.at[s],
            device_id=(a, across),
            device_id_type=MESH,
        )

    def send_half(s, passed):
        @pl.when(diagonal)
        def _():
            part_across(s).wait_recv()
            low_on(s).wait_recv()

        @pl.when(jnp.logical_not(diagonal))
        def _():
            part_arrival(s).wait_recv()

        @pl.loop(0, virt // chunk)
        def _(r):
            at = pl.ds(pl.multiple_of(r * chunk, chunk), chunk)
            rest = half[s, at, :] - part_in[s, at, :].astype(F32)
            half[s, at, :] = rest
            turned[s, :, at] = rest.T.astype(BF16)

        if passed:
            pass_on().start()
        else:

            @pl.when(a * rows + s != j)
            def _():
                mirror_copy(s).start()

    steps = rows * tiles
    half_at, late_at = tiles + 1, steps - 1
    early = slot == 0

    @pl.loop(0, steps)
    def _(step):
        s = lax.rem(j + step // tiles, rows)
        q = lax.rem(step, tiles)
        at_q = pl.ds(pl.multiple_of(q * tile, tile), tile)

        for turn in range(rows):

            @pl.when(step == 1 + 2 * turn)
            def _():
                relay(turn)

            @pl.when(jnp.logical_and(step == 4 + 2 * turn, diagonal))
            def _():
                low_to_flip(turn).wait_recv()
                low_on(turn).start()

            @pl.when(step == 2 + 2 * turn)
            def _():
                partial_sums(turn)

        sends = jnp.logical_or(
            jnp.logical_and(step == half_at, early),
            jnp.logical_and(step == late_at, jnp.logical_not(early)),
        )

        @pl.when(jnp.logical_and(sends, jnp.logical_not(diagonal)))
        def _():
            send_half(slot, True)

        @pl.when(jnp.logical_and(step == late_at, jnp.logical_and(diagonal, early)))
        def _():
            pass_on().wait_recv()
            pass_end().start()
            send_half(slot, False)

        first[...] = jnp.dot(
            pool[s, mine], x[:, at_q], preferred_element_type=F32
        ).astype(BF16)

        @pl.loop(0, tiles)
        def _(p):
            at_p = pl.ds(pl.multiple_of(p * tile, tile), tile)
            middle = jnp.dot(xt[at_p, :], first[...], preferred_element_type=F32)
            scaled[at_p, :] = (core[at_p, at_q].astype(F32) * middle).astype(BF16)

        second = jnp.dot(x[...], scaled[...], preferred_element_type=F32).astype(BF16)
        half[s] += lax.dot_general(
            second, x[:, at_q], (((1,), (1,)), ((), ())), preferred_element_type=F32
        )

    @pl.when(jnp.logical_and(diagonal, jnp.logical_not(early)))
    def _():
        pass_on().wait_recv()
        pass_end().start()
        send_half(slot, False)

    @pl.loop(1, rows)
    def _(t):
        send_half(lax.rem(j + t, rows), False)

    @pl.loop(0, rows)
    def _(t):
        s = lax.rem(j + t, rows)
        local = a * rows + s == j

        def finish(source):
            @pl.loop(0, virt // chunk)
            def _(r):
                at = pl.ds(pl.multiple_of(r * chunk, chunk), chunk)
                total = half[s, at, :] + source[s, at, :].astype(F32)
                residual_ref[s, at, :] = total
                column = jnp.broadcast_to(row_ref[:, at], (chunk, chunk)).T[:, :1]
                denominator = column + row_ref[...] - eps_ref[a * rows + s] - eps_ref[j]
                updated_ref[s, at, :] = (
                    pool[s, mine, at, :].astype(F32) - total / denominator
                ).astype(BF16)

        @pl.when(local)
        def _():
            finish(turned)

        @pl.when(jnp.logical_not(local))
        def _():
            mirror_arrival(s).wait_recv()
            finish(mirror)
            mirror_copy(s).wait_send()

    for s in range(rows):
        for d in far:
            gather_copy(s, d).wait_send()
            relay_copy(s, d).wait_send()
        partner_copy(s).wait_send()

    @pl.when(diagonal)
    def _():
        pass_end().wait_send()
        for s in range(rows):
            part_turned(s).wait_send()
            low_on(s).wait_send()

    @pl.when(jnp.logical_not(diagonal))
    def _():
        for s in range(rows):
            part_across(s).wait_send()
            low_to_flip(s).wait_send()


def shards(
    amplitudes,
    exch_int,
    thc_factor,
    thc_core,
    fock_vir,
    eps_vir,
    eps_occ,
    fock_occ,
    couple_list,
    couple_count,
):
    rows = amplitudes.shape[0]
    virt = amplitudes.shape[2]
    rank = thc_factor.shape[1]
    n_first = lax.axis_size("occi")
    n_second = lax.axis_size("occj")
    anywhere = pl.BlockSpec(memory_space=pl.ANY)
    vmem = pl.BlockSpec(memory_space=pltpu.VMEM)
    smem = pl.BlockSpec(memory_space=pltpu.SMEM)
    tile = tile_of(rank)
    pair = (rows, virt, virt)
    dma = pltpu.SemaphoreType.DMA
    residual, updated = pl.pallas_call(
        functools.partial(kernel, n_first, n_second),
        out_shape=(jax.ShapeDtypeStruct(pair, F32), jax.ShapeDtypeStruct(pair, BF16)),
        in_specs=[anywhere] * 5 + [vmem] + [smem] * 4,
        out_specs=(vmem, vmem),
        scratch_shapes=[
            pltpu.VMEM((rows, n_second // 2, virt, virt), BF16),
            pltpu.VMEM(pair, BF16),
            pltpu.VMEM((virt, rank), BF16),
            pltpu.VMEM((rank, virt), BF16),
            pltpu.VMEM((rank, rank), BF16),
            pltpu.VMEM((virt, virt), BF16),
            pltpu.VMEM((virt, tile), BF16),
            pltpu.VMEM((rank, tile), BF16),
            pltpu.VMEM(pair, F32),
            pltpu.VMEM(pair, BF16),
            pltpu.VMEM(pair, BF16),
            pltpu.VMEM(pair, BF16),
            pltpu.VMEM(pair, BF16),
            pltpu.VMEM((virt, virt), BF16),
            pltpu.VMEM((rows, virt // 2, virt), BF16),
            dma((4 + rows,)),
            dma((rows, n_second // 2)),
            dma((rows, n_second // 2)),
            dma((rows, n_second // 2)),
            dma((rows,)),
            dma((rows,)),
            dma((rows,)),
            dma((rows,)),
            dma((2,)),
            dma((rows,)),
            dma((rows,)),
            dma((rows,)),
            dma((rows,)),
        ],
        compiler_params=pltpu.CompilerParams(
            collective_id=0, has_side_effects=True, vmem_limit_bytes=60 * 1024 * 1024
        ),
    )(
        amplitudes.reshape(pair),
        exch_int.reshape(pair),
        thc_factor,
        thc_core,
        fock_vir,
        eps_vir.reshape(1, virt),
        eps_occ,
        fock_occ,
        couple_list,
        couple_count,
    )
    return (residual.reshape(rows, 1, virt, virt), updated.reshape(rows, 1, virt, virt))


def solution(mesh):
    placed = (P("occi", "occj", None, None),) * 2 + (P(),) * 8
    return jax.shard_map(
        shards,
        mesh=mesh,
        in_specs=placed,
        out_specs=(P("occi", "occj", None, None), P("occi", "occj", None, None)),
        check_vma=False,
    )
```

```python
import functools

import jax
import jax.numpy as jnp
from jax import lax
from jax.experimental import pallas as pl
from jax.experimental.pallas import tpu as pltpu
from jax.sharding import PartitionSpec as P

MESH = pl.DeviceIdType.MESH
F32 = jnp.float32
BF16 = jnp.bfloat16


def tile_of(extent):
    return 512 if extent % 512 == 0 else extent


def kernel(
    n_first,
    n_second,
    amp_hbm,
    int_hbm,
    x_hbm,
    core_hbm,
    fock_hbm,
    row_ref,
    eps_ref,
    fock_occ_ref,
    list_ref,
    count_ref,
    residual_ref,
    updated_ref,
    pool,
    integral,
    x,
    xt,
    core,
    fock,
    first,
    scaled,
    half,
    part_out,
    part_in,
    turned,
    mirror,
    passing,
    part_pass,
    local_sem,
    gsend_sem,
    grecv_sem,
    relay_sem,
    psend_sem,
    precv_sem,
    msend_sem,
    mrecv_sem,
    pass_sem,
    low_send_sem,
    low_recv_sem,
    low_pass_sem,
    low_done_sem,
):
    rows, virt = half.shape[0], half.shape[1]
    rank = x.shape[1]
    near = n_second // 2
    upper = pl.ds(0, virt // 2)
    lower = pl.ds(virt // 2, virt // 2)
    tile = tile_of(rank)
    tiles = rank // tile
    chunk = 128
    a = lax.axis_index("occi")
    j = lax.axis_index("occj")
    mine = lax.rem(j, near)
    base = j - mine
    across = lax.rem(j + near, n_second)
    i_half = a // (n_first // 2)
    diagonal = i_half == j // near
    partner = mine + 1 - 2 * lax.rem(mine, 2)
    slot = lax.rem(j, rows)
    flipped = lax.rem(a + n_first // 2, n_first)

    def weight(orbital, k):
        hits = jnp.float32(0.0)
        for entry in range(list_ref.shape[1]):
            active = jnp.logical_and(
                list_ref[orbital, entry] == k, entry < count_ref[orbital]
            )
            hits = hits + jnp.where(active, jnp.float32(1.0), jnp.float32(0.0))
        return hits * fock_occ_ref[orbital, k]

    def signal(first_coord, second_coord):
        pl.semaphore_signal(
            pltpu.get_barrier_semaphore(),
            inc=1,
            device_id=(first_coord, second_coord),
            device_id_type=MESH,
        )

    for d in range(1, near):
        signal(a, base + lax.rem(mine + d, near))
    signal(a, across)
    signal(flipped, j)
    signal(flipped, across)
    for s in range(rows):
        pair_i = a * rows + s

        @pl.when(diagonal)
        def _():
            signal(across // rows, pair_i)

        @pl.when(jnp.logical_not(diagonal))
        def _():
            signal(j // rows, lax.rem(pair_i + near, n_second))

        @pl.when(pair_i != j)
        def _():
            signal(j // rows, pair_i)

    @pl.when(diagonal)
    def _():
        signal(j // rows, flipped * rows + slot)

    @pl.when(jnp.logical_not(diagonal))
    def _():
        signal(lax.rem(j // rows + n_first // 2, n_first), a * rows + slot)

    loads = [
        pltpu.make_async_copy(x_hbm, x, local_sem.at[0]),
        pltpu.make_async_copy(fock_hbm, fock, local_sem.at[1]),
        pltpu.make_async_copy(int_hbm, integral, local_sem.at[2]),
        pltpu.make_async_copy(core_hbm, core, local_sem.at[3]),
    ]
    own_loads = [
        pltpu.make_async_copy(amp_hbm.at[s], pool.at[s, mine], local_sem.at[4 + s])
        for s in range(rows)
    ]
    for load in own_loads + loads:
        load.start()
    self_pair = a == j // rows
    greeted = near + 2 * rows + 3

    @pl.when(self_pair)
    def _():
        pl.semaphore_wait(pltpu.get_barrier_semaphore(), greeted - 1)

    @pl.when(jnp.logical_not(self_pair))
    def _():
        pl.semaphore_wait(pltpu.get_barrier_semaphore(), greeted)

    def gather_copy(s, d):
        peer = lax.rem(mine + d, near)
        return pltpu.make_async_remote_copy(
            src_ref=amp_hbm.at[s],
            dst_ref=pool.at[s, mine],
            send_sem=gsend_sem.at[s, d],
            recv_sem=grecv_sem.at[s, mine],
            device_id=(a, base + peer),
            device_id_type=MESH,
        )

    def partner_copy(s):
        return pltpu.make_async_remote_copy(
            src_ref=amp_hbm.at[s],
            dst_ref=pool.at[s, mine],
            send_sem=gsend_sem.at[s, 0],
            recv_sem=grecv_sem.at[s, mine],
            device_id=(a, base + partner),
            device_id_type=MESH,
        )

    def arrived(s, origin):
        pltpu.make_async_remote_copy(
            src_ref=amp_hbm.at[s],
            dst_ref=pool.at[s, origin],
            send_sem=gsend_sem.at[s, 0],
            recv_sem=grecv_sem.at[s, origin],
            device_id=(a, base + partner),
            device_id_type=MESH,
        ).wait_recv()

    def relay_copy(s, d):
        origin = lax.rem(mine + d, near)
        return pltpu.make_async_remote_copy(
            src_ref=pool.at[s, origin],
            dst_ref=pool.at[s, origin],
            send_sem=relay_sem.at[s, d],
            recv_sem=grecv_sem.at[s, origin],
            device_id=(a, base + partner),
            device_id_type=MESH,
        )

    far = range(2, near, 2)
    for s in range(rows):
        for d in far:
            gather_copy(s, d).start()
        partner_copy(s).start()

    loads[0].wait()
    for r in range(0, rank, tile):
        xt[pl.ds(r, tile), :] = x[:, pl.ds(r, tile)].T
    for load in own_loads + loads[1:3]:
        load.wait()
    for s in range(rows):
        half[s] = integral[s].astype(F32) + jnp.dot(
            fock[...], pool[s, mine], preferred_element_type=F32
        )
    loads[3].wait()

    def relay(s):
        for d in far:
            arrived(s, lax.rem(mine + d, near))
            relay_copy(s, d).start()

    def part_across(s):
        return pltpu.make_async_remote_copy(
            src_ref=part_out.at[s, upper],
            dst_ref=part_in.at[s, upper],
            send_sem=psend_sem.at[s],
            recv_sem=precv_sem.at[s],
            device_id=(a, across),
            device_id_type=MESH,
        )

    def part_turned(s):
        there = lax.rem(across, rows)
        return pltpu.make_async_remote_copy(
            src_ref=part_out.at[s],
            dst_ref=part_in.at[there],
            send_sem=psend_sem.at[s],
            recv_sem=precv_sem.at[there],
            device_id=(across // rows, a * rows + s),
            device_id_type=MESH,
        )

    def low_to_flip(s):
        return pltpu.make_async_remote_copy(
            src_ref=part_out.at[s, lower],
            dst_ref=part_pass.at[s],
            send_sem=low_send_sem.at[s],
            recv_sem=low_recv_sem.at[s],
            device_id=(flipped, j),
            device_id_type=MESH,
        )

    def low_on(s):
        return pltpu.make_async_remote_copy(
            src_ref=part_pass.at[s],
            dst_ref=part_in.at[s, lower],
            send_sem=low_pass_sem.at[s],
            recv_sem=low_done_sem.at[s],
            device_id=(flipped, across),
            device_id_type=MESH,
        )

    def partial_sums(s):
        arrived(s, base * 0 + partner)
        for d in far:
            arrived(s, lax.rem(partner + near + d, near))

        own_weights = [weight(j, base + k) for k in range(near)]
        other_weights = [weight(across, base + k) for k in range(near)]

        @pl.loop(0, virt // chunk)
        def _(r):
            at = pl.ds(pl.multiple_of(r * chunk, chunk), chunk)
            own = jnp.zeros((chunk, virt), F32)
            other = jnp.zeros((chunk, virt), F32)
            for k in range(near):
                block = pool[s, k, at, :].astype(F32)
                own = own + own_weights[k] * block
                other = other + other_weights[k] * block
            half[s, at, :] = half[s, at, :] - own

            @pl.when(diagonal)
            def _():
                part_out[s, :, at] = other.T.astype(BF16)

            @pl.when(jnp.logical_not(diagonal))
            def _():
                part_out[s, at, :] = other.astype(BF16)

        @pl.when(diagonal)
        def _():
            part_turned(s).start()

        @pl.when(jnp.logical_not(diagonal))
        def _():
            low_to_flip(s).start()
            part_across(s).start()

    def mirror_copy(s):
        return pltpu.make_async_remote_copy(
            src_ref=turned.at[s],
            dst_ref=mirror.at[slot],
            send_sem=msend_sem.at[s],
            recv_sem=mrecv_sem.at[slot],
            device_id=(j // rows, a * rows + s),
            device_id_type=MESH,
        )

    def pass_on():
        return pltpu.make_async_remote_copy(
            src_ref=turned.at[slot],
            dst_ref=passing,
            send_sem=msend_sem.at[slot],
            recv_sem=pass_sem.at[0],
            device_id=(flipped, j),
            device_id_type=MESH,
        )

    def pass_end():
        return pltpu.make_async_remote_copy(
            src_ref=passing,
            dst_ref=mirror.at[slot],
            send_sem=pass_sem.at[1],
            recv_sem=mrecv_sem.at[slot],
            device_id=(j // rows, flipped * rows + slot),
            device_id_type=MESH,
        )

    def mirror_arrival(s):
        return pltpu.make_async_remote_copy(
            src_ref=turned.at[s],
            dst_ref=mirror.at[s],
            send_sem=msend_sem.at[s],
            recv_sem=mrecv_sem.at[s],
            device_id=(j // rows, a * rows + s),
            device_id_type=MESH,
        )

    def part_arrival(s):
        return pltpu.make_async_remote_copy(
            src_ref=part_out.at[s],
            dst_ref=part_in.at[s],
            send_sem=psend_sem.at[s],
            recv_sem=precv_sem.at[s],
            device_id=(a, across),
            device_id_type=MESH,
        )

    def send_half(s, passed):
        @pl.when(diagonal)
        def _():
            part_across(s).wait_recv()
            low_on(s).wait_recv()

        @pl.when(jnp.logical_not(diagonal))
        def _():
            part_arrival(s).wait_recv()

        @pl.loop(0, virt // chunk)
        def _(r):
            at = pl.ds(pl.multiple_of(r * chunk, chunk), chunk)
            rest = half[s, at, :] - part_in[s, at, :].astype(F32)
            half[s, at, :] = rest
            turned[s, :, at] = rest.T.astype(BF16)

        if passed:
            pass_on().start()
        else:

            @pl.when(a * rows + s != j)
            def _():
                mirror_copy(s).start()

    steps = rows * tiles
    half_at, late_at = tiles + 1, steps - 1
    early = slot == 0

    @pl.loop(0, steps)
    def _(step):
        s = lax.rem(j + step // tiles, rows)
        q = lax.rem(step, tiles)
        at_q = pl.ds(pl.multiple_of(q * tile, tile), tile)

        for turn in range(rows):

            @pl.when(step == 1 + 2 * turn)
            def _():
                relay(turn)

            @pl.when(jnp.logical_and(step == 4 + 2 * turn, diagonal))
            def _():
                low_to_flip(turn).wait_recv()
                low_on(turn).start()

            @pl.when(step == 2 + 2 * turn)
            def _():
                partial_sums(turn)

        sends = jnp.logical_or(
            jnp.logical_and(step == half_at, early),
            jnp.logical_and(step == late_at, jnp.logical_not(early)),
        )

        @pl.when(jnp.logical_and(sends, jnp.logical_not(diagonal)))
        def _():
            send_half(slot, True)

        @pl.when(jnp.logical_and(step == late_at, jnp.logical_and(diagonal, early)))
        def _():
            send_half(slot, False)
            pass_on().wait_recv()
            pass_end().start()

        first[...] = jnp.dot(
            pool[s, mine], x[:, at_q], preferred_element_type=F32
        ).astype(BF16)

        @pl.loop(0, tiles)
        def _(p):
            at_p = pl.ds(pl.multiple_of(p * tile, tile), tile)
            middle = jnp.dot(xt[at_p, :], first[...], preferred_element_type=F32)
            scaled[at_p, :] = (core[at_p, at_q].astype(F32) * middle).astype(BF16)

        second = jnp.dot(x[...], scaled[...], preferred_element_type=F32).astype(BF16)
        half[s] += lax.dot_general(
            second, x[:, at_q], (((1,), (1,)), ((), ())), preferred_element_type=F32
        )

    @pl.when(jnp.logical_and(diagonal, jnp.logical_not(early)))
    def _():
        send_half(slot, False)

    @pl.loop(1, rows)
    def _(t):
        send_half(lax.rem(j + t, rows), False)

    @pl.when(jnp.logical_and(diagonal, jnp.logical_not(early)))
    def _():
        pass_on().wait_recv()
        pass_end().start()

    @pl.loop(0, rows)
    def _(t):
        s = lax.rem(j + t, rows)
        local = a * rows + s == j

        def finish(source):
            @pl.loop(0, virt // chunk)
            def _(r):
                at = pl.ds(pl.multiple_of(r * chunk, chunk), chunk)
                total = half[s, at, :] + source[s, at, :].astype(F32)
                residual_ref[s, at, :] = total
                column = jnp.broadcast_to(row_ref[:, at], (chunk, chunk)).T[:, :1]
                denominator = column + row_ref[...] - eps_ref[a * rows + s] - eps_ref[j]
                updated_ref[s, at, :] = (
                    pool[s, mine, at, :].astype(F32) - total / denominator
                ).astype(BF16)

        @pl.when(local)
        def _():
            finish(turned)

        @pl.when(jnp.logical_not(local))
        def _():
            mirror_arrival(s).wait_recv()
            finish(mirror)
            mirror_copy(s).wait_send()

    for s in range(rows):
        for d in far:
            gather_copy(s, d).wait_send()
            relay_copy(s, d).wait_send()
        partner_copy(s).wait_send()

    @pl.when(diagonal)
    def _():
        pass_end().wait_send()
        for s in range(rows):
            part_turned(s).wait_send()
            low_on(s).wait_send()

    @pl.when(jnp.logical_not(diagonal))
    def _():
        for s in range(rows):
            part_across(s).wait_send()
            low_to_flip(s).wait_send()


def shards(
    amplitudes,
    exch_int,
    thc_factor,
    thc_core,
    fock_vir,
    eps_vir,
    eps_occ,
    fock_occ,
    couple_list,
    couple_count,
):
    rows = amplitudes.shape[0]
    virt = amplitudes.shape[2]
    rank = thc_factor.shape[1]
    n_first = lax.axis_size("occi")
    n_second = lax.axis_size("occj")
    anywhere = pl.BlockSpec(memory_space=pl.ANY)
    vmem = pl.BlockSpec(memory_space=pltpu.VMEM)
    smem = pl.BlockSpec(memory_space=pltpu.SMEM)
    tile = tile_of(rank)
    pair = (rows, virt, virt)
    dma = pltpu.SemaphoreType.DMA
    residual, updated = pl.pallas_call(
        functools.partial(kernel, n_first, n_second),
        out_shape=(jax.ShapeDtypeStruct(pair, F32), jax.ShapeDtypeStruct(pair, BF16)),
        in_specs=[anywhere] * 5 + [vmem] + [smem] * 4,
        out_specs=(vmem, vmem),
        scratch_shapes=[
            pltpu.VMEM((rows, n_second // 2, virt, virt), BF16),
            pltpu.VMEM(pair, BF16),
            pltpu.VMEM((virt, rank), BF16),
            pltpu.VMEM((rank, virt), BF16),
            pltpu.VMEM((rank, rank), BF16),
            pltpu.VMEM((virt, virt), BF16),
            pltpu.VMEM((virt, tile), BF16),
            pltpu.VMEM((rank, tile), BF16),
            pltpu.VMEM(pair, F32),
            pltpu.VMEM(pair, BF16),
            pltpu.VMEM(pair, BF16),
            pltpu.VMEM(pair, BF16),
            pltpu.VMEM(pair, BF16),
            pltpu.VMEM((virt, virt), BF16),
            pltpu.VMEM((rows, virt // 2, virt), BF16),
            dma((4 + rows,)),
            dma((rows, n_second // 2)),
            dma((rows, n_second // 2)),
            dma((rows, n_second // 2)),
            dma((rows,)),
            dma((rows,)),
            dma((rows,)),
            dma((rows,)),
            dma((2,)),
            dma((rows,)),
            dma((rows,)),
            dma((rows,)),
            dma((rows,)),
        ],
        compiler_params=pltpu.CompilerParams(
            collective_id=0, has_side_effects=True, vmem_limit_bytes=60 * 1024 * 1024
        ),
    )(
        amplitudes.reshape(pair),
        exch_int.reshape(pair),
        thc_factor,
        thc_core,
        fock_vir,
        eps_vir.reshape(1, virt),
        eps_occ,
        fock_occ,
        couple_list,
        couple_count,
    )
    return (residual.reshape(rows, 1, virt, virt), updated.reshape(rows, 1, virt, virt))


def solution(mesh):
    placed = (P("occi", "occj", None, None),) * 2 + (P(),) * 8
    return jax.shard_map(
        shards,
        mesh=mesh,
        in_specs=placed,
        out_specs=(P("occi", "occj", None, None), P("occi", "occj", None, None)),
        check_vma=False,
    )
```
